32 devices in a mesh: groups: 2 (over y), dp: 4 (over x, core), tensor: 4 (over z).
Axes of the slice: x: 2, y: 2, z: 4, core: 2. Of those that a mesh axis runs over, the one named last changes fastest.
Arguments:
- tokens: bfloat16 [4096, 4096], P(('groups', 'dp'), 'tensor'), parts along dimension 0, may hold values from -6 to 6
- cotangent: bfloat16 [4096, 4096], P(('groups', 'dp'), 'tensor'), parts along dimension 0, may hold values from -6 to 6
- expert_ids: int32 [4096, 2], P(('groups', 'dp')), parts along dimension 0, may hold values from 0 to 7, as said below
- gate_prob: float32 [4096, 2], P(('groups', 'dp')), parts along dimension 0, may hold values from 0.25 to 1
- row_token: int32 [2048], P(('groups', 'dp')), parts along dimension 0, may hold values from 0 to 512, as said below
- w_hidden: bfloat16 [4096, 14336], P('dp', 'tensor'), may hold values from -0.125 to 0.125
- w_output: bfloat16 [14336, 4096], P('tensor', 'dp'), may hold values from -0.0625 to 0.0625
Outputs:
- output: bfloat16 [4096, 4096], P(('groups', 'dp'), 'tensor'), parts along dimension 0
- grad_tokens: bfloat16 [4096, 4096], P(('groups', 'dp'), 'tensor'), parts along dimension 0
- grad_hidden: float32 [8192, 14336], P(('groups', 'dp'), 'tensor'), parts along dimension 0
- grad_output: float32 [28672, 4096], P(('groups', 'tensor'), 'dp'), parts along dimension 0
The draws below stay inside these ranges and needn't reach their ends.
There are 2 independent parts, one for each index of `groups`. The reference program is written for one: setup_inputs(seed, part) draws one part's arguments, and reference() takes and returns one part's arrays. A program takes and returns all parts, laid end to end along the dimension named above; an argument that names none is the same for every part. Nothing has to cross between parts.
Inputs may be any that keep to these rules, and one draw needn't show every extreme that they name: `expert_ids`: each token names two different experts; expert 0 is named by exactly the tokens that row_token lists. `row_token`: in each aligned block of 256 entries (one block per index of dp) the entries are the local indices of that index's tokens that name expert 0, rising, followed by 512 in the remaining entries. In every draw some block has no entry 512 and some block lists at most 128 tokens.
All inputs are finite; a program needn't handle non-finite values.
Results may differ from the reference program's by a relative error of at most 0.012.
Values may be sent and summed in bfloat16 or wider, within the bound.
A program may use at most 256 MiB of HBM per device.

```python
import jax
import jax.numpy as jnp
from jax import lax

D = 4096
EXPERTS = 8
FF = 14336
TOK_DEV = 512
BLOCK = 128
ROWS = 256
TOKENS = 2048
N_DP = 4
N_TENSOR = 4


def routing_tables(key):
    base = jax.random.fold_in(key, 7)
    count_key, small_key, order_key, perm_key, slot_key, first_key, second_key = jax.random.split(base, 7)
    counts = jax.random.randint(count_key, (N_DP,), ROWS // 8, ROWS + 1)
    order = jax.random.permutation(order_key, N_DP)
    counts = counts.at[order[0]].set(ROWS)
    small_count = jax.random.randint(small_key, (), ROWS // 8, BLOCK + 1)
    counts = counts.at[order[1]].set(small_count)
    perm_keys = jax.random.split(perm_key, N_DP)
    perms = jax.vmap(lambda single: jax.random.permutation(single, TOK_DEV))(perm_keys)
    ranks = jnp.argsort(perms, axis=1)
    member = ranks < counts[:, None]
    position = jnp.cumsum(member.astype(jnp.int32), axis=1) - 1
    target = jnp.where(member, position, ROWS).astype(jnp.int32)
    table = jnp.full((N_DP, ROWS + 1), TOK_DEV, jnp.int32)
    device_rows = jnp.broadcast_to(jnp.arange(N_DP, dtype=jnp.int32)[:, None], (N_DP, TOK_DEV))
    token_index = jnp.broadcast_to(jnp.arange(TOK_DEV, dtype=jnp.int32)[None, :], (N_DP, TOK_DEV))
    table = table.at[device_rows, target].set(token_index)
    row_table = table[:, :ROWS].reshape(-1)
    flat_member = member.reshape(-1)
    slot = jax.random.randint(slot_key, (N_DP * TOK_DEV,), 0, 2)
    first = jax.random.randint(first_key, (N_DP * TOK_DEV,), 1, EXPERTS)
    second = 1 + (first - 1 + jax.random.randint(second_key, (N_DP * TOK_DEV,), 1, EXPERTS - 1)) % (EXPERTS - 1)
    column_one = jnp.where(flat_member & (slot == 0), 0, first)
    column_two = jnp.where(flat_member & (slot == 1), 0, jnp.where(flat_member, first, second))
    id_table = jnp.stack([column_one, column_two], axis=1).astype(jnp.int32)
    return (id_table, row_table)


def draw_expert_ids(key, part):
    return routing_tables(key)[0]


def draw_row_token(key, part):
    return routing_tables(key)[1]


def spiked(values, rng, source, target, shards_of, factor):
    owner, partner = [(jnp.arange(values.shape[dim]) // (values.shape[dim] // shards_of)).reshape([-1 if axis == dim else 1 for axis in range(values.ndim)]) for dim in (source, target)]
    chosen = jax.random.permutation(rng, shards_of)[partner]
    strong = (owner == chosen) | (owner == (partner + shards_of // 2) % shards_of)
    return jnp.where(strong, factor * values, values)


def levels(key, shape, cuts, low, top_value):
    def one(dim, blocks):
        heights = jax.random.uniform(jax.random.fold_in(jax.random.fold_in(key, 6), dim), (blocks,), jnp.float32, low / len(cuts), top_value / len(cuts))
        return jnp.repeat(jnp.exp(heights), shape[dim] // blocks).reshape((-1,) + (1,) * (len(shape) - dim - 1))

    factor_of = one(*cuts[0])
    for cut in cuts[1:]:
        factor_of = factor_of * one(*cut)
    return factor_of


def scatter_about(own_key, extent, width, bound, cuts=(), held_as=jnp.bfloat16):
    entries = jax.random.normal(own_key, extent, jnp.float32) * width
    if len(cuts) > 0:
        entries = levels(own_key, extent, cuts, -0.22, 0.18) * entries
    return jnp.clip(entries, min=-bound, max=bound).astype(held_as)


def bell_draw_with(rng, dims, width, most, cuts, heavy, kind=jnp.bfloat16):
    result = width * jax.random.normal(rng, dims, jnp.float32)
    if cuts:
        result = result * levels(rng, dims, cuts, -0.22, 0.18)
    return jnp.clip(spiked(result, jax.random.fold_in(rng, 3), *heavy), -most, most).astype(kind)


def setup_inputs(seed: int = 0, part: int = 0) -> dict:
    splits = jax.random.split(jax.random.key(seed), 8)
    part_keys = jax.random.split(jax.random.fold_in(splits[7], part), 8)
    return {
        "tokens": scatter_about(part_keys[0], (TOKENS, D), 1.0, 6.0, ((0, 4), (1, 4))),
        "cotangent": scatter_about(part_keys[1], (TOKENS, D), 1.0, 6.0, ((0, 4), (1, 4))),
        "expert_ids": draw_expert_ids(jax.random.fold_in(jax.random.fold_in(splits[7], part), 71), part),
        "gate_prob": jnp.clip(0.25 + 0.75 * jax.random.uniform(part_keys[3], (TOKENS, 2), jnp.float32) ** levels(part_keys[3], (TOKENS, 2), ((0, 4),), -0.2, 0.2), 0.25, 1.0),
        "row_token": draw_row_token(jax.random.fold_in(jax.random.fold_in(splits[7], part), 71), part),
        "w_hidden": bell_draw_with(splits[5], (D, FF), D ** -0.5, 0.125, ((0, 4), (1, 4)), (1, 0, 4, 2.0)),
        "w_output": bell_draw_with(splits[6], (FF, D), FF ** -0.5, 0.0625, ((0, 4), (1, 4)), (0, 1, 4, 2.0)),
    }


def place_rows(values, target, total):
    buffer = jnp.zeros((total + 1, values.shape[1]), jnp.float32)
    return buffer.at[target].set(values)[:total].astype(jnp.bfloat16)


def grouped_sum(left, right):
    group_width = FF // N_TENSOR

    def add_group(running, group):
        begin = group * group_width
        left_part = lax.dynamic_slice_in_dim(left, begin, group_width, 1)
        right_part = lax.dynamic_slice_in_dim(right, begin, group_width, 0)
        product = jnp.dot(left_part, right_part, preferred_element_type=jnp.float32)
        rounded = lax.optimization_barrier(product.astype(jnp.bfloat16))
        return running + rounded.astype(jnp.float32), None

    initial = jnp.zeros((left.shape[0], right.shape[1]), jnp.float32)
    return lax.scan(add_group, initial, jnp.arange(N_TENSOR, dtype=jnp.int32))[0]


def reference(tokens, cotangent, expert_ids, gate_prob, row_token, w_hidden, w_output):
    weight = jnp.sum(jnp.where(expert_ids == 0, gate_prob, 0.0), axis=1)
    blocks = row_token.reshape(N_DP, ROWS)
    offsets = jnp.arange(N_DP, dtype=jnp.int32)[:, None] * TOK_DEV
    live = blocks < TOK_DEV
    source = jnp.where(live, blocks + offsets, 0).reshape(-1).astype(jnp.int32)
    target = jnp.where(live, blocks + offsets, TOKENS).reshape(-1).astype(jnp.int32)
    live_rows = live.reshape(-1)
    mask = live_rows[:, None]
    x_rows = jnp.where(mask, tokens[source], jnp.zeros((), tokens.dtype))
    dy_rows = jnp.where(mask, cotangent[source], jnp.zeros((), cotangent.dtype))
    p_rows = jnp.where(live_rows, weight[source], 0.0)
    pre = jnp.dot(x_rows, w_hidden, preferred_element_type=jnp.float32)
    hidden = jax.nn.silu(pre).astype(jnp.bfloat16)
    expert_out = grouped_sum(hidden, w_output)
    output = place_rows(p_rows[:, None] * expert_out, target, TOKENS)
    scaled = (p_rows[:, None] * dy_rows.astype(jnp.float32)).astype(jnp.bfloat16)
    d_hidden = lax.dot_general(scaled, w_output, (((1,), (1,)), ((), ())), preferred_element_type=jnp.float32)
    sig = jax.nn.sigmoid(pre)
    d_pre = (d_hidden * sig * (1.0 + pre * (1.0 - sig))).astype(jnp.bfloat16)
    d_rows = grouped_sum(d_pre, w_hidden.T)
    grad_tokens = place_rows(d_rows, target, TOKENS)
    grad_hidden = lax.dot_general(x_rows, d_pre, (((0,), (0,)), ((), ())), preferred_element_type=jnp.float32)
    grad_output = lax.dot_general(hidden, scaled, (((0,), (0,)), ((), ())), preferred_element_type=jnp.float32)
    return (output, grad_tokens, grad_hidden, grad_output)
```

```python
import jax
import jax.numpy as jnp
from jax import lax
from jax.sharding import PartitionSpec as P

F32 = jnp.float32
BF16 = jnp.bfloat16


def place_rows(values, target, total):
    buffer = jnp.zeros((total + 1, values.shape[1]), F32)
    return buffer.at[target].set(values)[:total].astype(BF16)


def chunk_count(width):
    for count in (7, 4, 2):
        if width % (count * 256) == 0:
            return count
    return 1


def transposed(n):
    return [(i * n + j, j * n + i) for i in range(n) for j in range(n)]


def to_columns(local, n_dp, n_tensor):
    if n_dp == n_tensor:
        swapped = lax.ppermute(local, ("dp", "tensor"), transposed(n_dp))
        return lax.all_gather(swapped, "tensor", axis=0, tiled=True)
    rows = lax.all_gather(local, "tensor", axis=1, tiled=True)
    return lax.all_to_all(rows, "dp", split_axis=1, concat_axis=0, tiled=True)


def to_tokens(partial, n_dp, n_tensor):
    if n_dp == n_tensor:
        summed = lax.psum_scatter(partial, "tensor", scatter_dimension=0, tiled=True)
        return lax.ppermute(summed, ("dp", "tensor"), transposed(n_dp))
    rows = lax.all_to_all(partial, "dp", split_axis=0, concat_axis=1, tiled=True)
    return lax.psum_scatter(rows, "tensor", scatter_dimension=1, tiled=True)


def swap(value, n_dp, bit):
    return lax.ppermute(value, "dp", [(i, i ^ (1 << bit)) for i in range(n_dp)])


def join(parts, axis=0):
    return parts[0] if len(parts) == 1 else jnp.concatenate(parts, axis)


def summed_over_dp(product, blocks, n_dp):
    bits = n_dp.bit_length() - 1
    kept = list(range(len(blocks)))
    total = None
    for bit in range(bits):
        if bit == bits - 1:
            mine = product(join([blocks[k] for k in kept])) if total is None else total
            return mine + swap(mine.astype(BF16), n_dp, bit).astype(F32)
        stay = kept[::2]
        go = kept[1::2]
        if total is None:
            sent = product(join([blocks[k] for k in go])).astype(BF16)
            mine = product(join([blocks[k] for k in stay]))
        else:
            split = total.reshape(len(stay), 2, -1, total.shape[1])
            sent = split[:, 1].reshape(-1, total.shape[1]).astype(BF16)
            mine = split[:, 0].reshape(-1, total.shape[1])
        total = mine + swap(sent, n_dp, bit).astype(F32)
        kept = stay
    return product(join(blocks))


def gathered_over_dp(own, n_dp):
    bits = n_dp.bit_length() - 1
    held = [own]
    for bit in reversed(range(bits - 1)):
        other = jnp.split(swap(join(held), n_dp, bit), len(held))
        held = [part for pair in zip(held, other) for part in pair]
    return join(held)


def body(tokens, cotangent, expert_ids, gate_prob, row_token, w_hidden, w_output):
    n_dp = lax.axis_size("dp")
    n_tensor = lax.axis_size("tensor")
    me = lax.axis_index("dp")
    tok_dev = tokens.shape[0]
    live = row_token < tok_dev
    source = jnp.where(live, row_token, 0)
    weight = jnp.sum(jnp.where(expert_ids == 0, gate_prob, 0.0), axis=1)
    p_rows = jnp.where(live, weight[source], 0.0)
    mask = live[:, None]
    x_local = jnp.where(mask, tokens[source], jnp.zeros((), BF16))
    dy_local = jnp.where(mask, cotangent[source], jnp.zeros((), BF16))
    scaled_local = (p_rows[:, None] * dy_local.astype(F32)).astype(BF16)
    n_blocks = max(n_dp // 2, 1)
    low = lax.rem(me, n_blocks)

    def relative(array):
        split = array.reshape(n_blocks, -1, array.shape[1])
        return [lax.dynamic_index_in_dim(split, low ^ k, 0, keepdims=False) for k in range(n_blocks)]

    x_blocks = relative(to_columns(x_local, n_dp, n_tensor))
    s_blocks = relative(to_columns(scaled_local, n_dp, n_tensor))
    width = w_hidden.shape[1]
    n_chunks = chunk_count(width)
    step = width // n_chunks
    pre, hidden_parts, d_pre_parts = [], [], []
    for c in range(n_chunks):
        w_part = w_hidden[:, c * step : (c + 1) * step]
        value = summed_over_dp(
            lambda rows: jnp.dot(rows, w_part, preferred_element_type=F32), x_blocks, n_dp
        )
        pre.append(value)
        hidden_parts.append(gathered_over_dp(jax.nn.silu(value).astype(BF16), n_dp))
    hidden = join(hidden_parts, 1)
    x_rel = join(x_blocks)
    s_rel = join(s_blocks)
    for c in range(n_chunks):
        w_part = w_output[c * step : (c + 1) * step]
        d_hidden = summed_over_dp(
            lambda rows: lax.dot_general(
                rows, w_part, (((1,), (1,)), ((), ())), preferred_element_type=F32
            ),
            s_blocks,
            n_dp,
        )
        sig = jax.nn.sigmoid(pre[c])
        own = (d_hidden * sig * (1.0 + pre[c] * (1.0 - sig))).astype(BF16)
        d_pre_parts.append(gathered_over_dp(own, n_dp))
    d_pre = join(d_pre_parts, 1)

    def absolute(array):
        return join(relative(array))

    out_part = jnp.dot(hidden, w_output, preferred_element_type=F32).astype(BF16)
    summed_out = to_tokens(absolute(out_part), n_dp, n_tensor).astype(F32)
    output = place_rows(summed_out * p_rows[:, None], row_token, tok_dev)
    in_part = lax.dot_general(
        d_pre, w_hidden, (((1,), (1,)), ((), ())), preferred_element_type=F32
    ).astype(BF16)
    summed_in = to_tokens(absolute(in_part), n_dp, n_tensor).astype(F32)
    grad_tokens = place_rows(summed_in, row_token, tok_dev)
    grad_output = lax.dot_general(
        hidden, s_rel, (((0,), (0,)), ((), ())), preferred_element_type=F32
    )
    grad_hidden = lax.dot_general(
        x_rel, d_pre, (((0,), (0,)), ((), ())), preferred_element_type=F32
    )
    return (output, grad_tokens, grad_hidden, grad_output)


def solution(mesh):
    return jax.shard_map(
        body,
        mesh=mesh,
        in_specs=(
            P(("groups", "dp"), "tensor"),
            P(("groups", "dp"), "tensor"),
            P(("groups", "dp"), None),
            P(("groups", "dp"), None),
            P(("groups", "dp")),
            P("dp", "tensor"),
            P("tensor", "dp"),
        ),
        out_specs=(
            P(("groups", "dp"), "tensor"),
            P(("groups", "dp"), "tensor"),
            P(("groups", "dp"), "tensor"),
            P(("groups", "tensor"), "dp"),
        ),
        check_vma=False,
    )
```
